512 devices in a mesh: node: 16 (over z), cuts: 32 (over x, y, core).
Axes of the slice: x: 4, y: 4, z: 16, core: 2. Of those that a mesh axis runs over, the one named last changes fastest.
Arguments:
- core_x: bfloat16 [32, 256, 256, 256], P('node', 'cuts'), may hold values from -6 to 6
- core_y: bfloat16 [32, 256, 256, 256], P('node', 'cuts'), may hold values from -0.0234375 to 0.0234375
- left_intersection: bfloat16 [32, 256, 256], P('node', 'cuts'), may hold values from -0.375 to 0.375
- right_intersection: bfloat16 [32, 256, 256], P('node', 'cuts'), may hold values from -0.375 to 0.375
Outputs:
- parent_intersection: float32 [32, 256, 256], P('node', 'cuts')
The draws below stay inside these ranges and needn't reach their ends.
All inputs are finite; a program needn't handle non-finite values.
Results may differ from the reference program's by a relative error of at most 0.004.
Values may be sent and summed in bfloat16 or wider, within the bound.
A program may use at most 64 MiB of HBM per device.

```python
import jax
import jax.numpy as jnp
from jax import lax

R = 256
PARENTS = 32


def block_scale(stream_key, shape, shards, low, high):
    gain, own = 1.0, jax.random.fold_in(stream_key, 6)
    for position, blocks in shards:
        steps = jnp.exp(jax.random.uniform(jax.random.fold_in(own, position), (blocks,), jnp.float32, low / len(shards), high / len(shards)))
        gain = gain * jnp.repeat(steps, shape[position] // blocks).reshape([-1 if axis == position else 1 for axis in range(len(shape))])
    return gain


def gaussian(own_key, extent, deviation, reach, pieces=(), dtype=jnp.bfloat16):
    values = deviation * jax.random.normal(own_key, extent, jnp.float32)
    if pieces:
        values = values * block_scale(own_key, extent, pieces, -0.22, 0.18)
    return jnp.clip(values, -reach, reach).astype(dtype)


def setup_inputs(seed: int = 0) -> dict:
    streams_of = jax.random.split(jax.random.key(seed), 5)
    return {
        "core_x": gaussian(streams_of[0], (PARENTS, R, R, R), 1.0, 6.0, ((0, 16), (1, 32))),
        "core_y": gaussian(streams_of[1], (PARENTS, R, R, R), (R * R) ** -0.5, 0.0234375, ((0, 16), (1, 32))),
        "left_intersection": gaussian(streams_of[2], (PARENTS, R, R), R ** -0.5, 0.375, ((0, 16), (1, 32))),
        "right_intersection": gaussian(streams_of[3], (PARENTS, R, R), R ** -0.5, 0.375, ((0, 16), (1, 32))),
    }


def one_parent(items):
    block_x, block_y, left_mat, right_mat = items
    first = jnp.einsum("ik,aij->akj", left_mat.astype(jnp.float32), block_x.astype(jnp.float32)).astype(jnp.bfloat16)
    second = jnp.einsum("akj,jl->akl", first.astype(jnp.float32), right_mat.astype(jnp.float32)).astype(jnp.bfloat16)
    return jnp.einsum("akl,klb->ab", second.astype(jnp.float32), block_y.astype(jnp.float32))


def reference(core_x, core_y, left_intersection, right_intersection):
    return lax.map(one_parent, (core_x, core_y, left_intersection, right_intersection))
```

```python
import jax
import jax.numpy as jnp
from jax import lax
from jax.experimental import pallas as pl
from jax.experimental.pallas import tpu as pltpu
from jax.sharding import PartitionSpec as P

MESH = pl.DeviceIdType.MESH
SIDE = 4
CHIPS = SIDE * SIDE
OFFSETS = (
    (2, 2),
    (2, 1),
    (2, 3),
    (1, 2),
    (3, 2),
    (1, 1),
    (3, 3),
    (1, 3),
    (3, 1),
    (2, 0),
    (0, 2),
    (1, 0),
    (3, 0),
    (0, 1),
    (0, 3),
)
GROUP = 4


def kernel(
    x_hbm,
    y_hbm,
    l_hbm,
    r_hbm,
    o_ref,
    xv,
    yv,
    lv,
    rv,
    lt,
    tv,
    rc,
    sc,
    part,
    ret,
    local,
    pair_send,
    pair_recv,
    l_send,
    l_recv,
    r_send,
    r_recv,
    t_send,
    t_recv,
    b_send,
    b_recv,
):
    parents, rows = x_hbm.shape[0], x_hbm.shape[1]
    rank = x_hbm.shape[2]
    per_chip = 2 * rows
    me = lax.axis_index("cuts")
    h = me % 2
    chip = me // 2
    x, y = chip // SIDE, chip % SIDE

    def chip_at(dx, dy):
        return ((x + dx) % SIDE) * SIDE + (y + dy) % SIDE

    def remote(src, dst, send, recv, device):
        return pltpu.make_async_remote_copy(
            src_ref=src,
            dst_ref=dst,
            send_sem=send,
            recv_sem=recv,
            device_id={"cuts": device},
            device_id_type=MESH,
        )

    partner = chip * 2 + 1 - h
    ahead = [chip_at(dx, dy) for dx, dy in OFFSETS]
    behind = [chip_at(SIDE - dx, SIDE - dy) for dx, dy in OFFSETS]

    own_l = pltpu.make_async_copy(l_hbm, lv.at[:, chip, h], local.at[0])
    own_r = pltpu.make_async_copy(r_hbm, rv.at[:, chip, h], local.at[1])
    own_x = pltpu.make_async_copy(x_hbm, xv, local.at[2])
    own_y = pltpu.make_async_copy(y_hbm, yv.at[:, h], local.at[3])
    for copy in (own_l, own_r, own_x, own_y):
        copy.start()

    barrier = pltpu.get_barrier_semaphore()
    for c in ahead:
        pl.semaphore_signal(
            barrier, inc=1, device_id={"cuts": 2 * c + h}, device_id_type=MESH
        )
    pl.semaphore_signal(
        barrier, inc=1, device_id={"cuts": partner}, device_id_type=MESH
    )
    pl.semaphore_wait(barrier, CHIPS)

    def spread(ref, send, recv):
        mine = ref.at[:, chip, h]
        return [
            remote(mine, mine, send.at[o], recv.at[o], 2 * c + h)
            for o, c in enumerate(ahead)
        ]

    l_copies = spread(lv, l_send, l_recv)
    r_copies = spread(rv, r_send, r_recv)
    own_l.wait()
    for copy in l_copies:
        copy.start()
    own_r.wait()
    for copy in r_copies:
        copy.start()
    y_pair = remote(y_hbm, yv.at[:, h], pair_send.at[0], pair_recv.at[0], partner)
    y_pair.start()

    def landed(ref, recv, o):
        theirs = ref.at[:, behind[o], h]
        return remote(theirs, theirs, l_send.at[o], recv.at[o], 2 * ahead[o] + h)

    for o in range(CHIPS - 1):
        landed(lv, l_recv, o).wait_recv()
    l_pair = remote(
        lv.at[:, :, h], lv.at[:, :, h], pair_send.at[1], pair_recv.at[1], partner
    )
    l_pair.start()
    own_x.wait()
    l_pair.wait_recv()

    def piece(p, o):
        return remote(
            tv.at[p, ahead[o]],
            rc.at[p, o + 1],
            t_send.at[p, o],
            t_recv.at[p, o],
            2 * ahead[o] + h,
        )

    def give(p, o):
        return remote(
            part.at[p, o + 1],
            ret.at[p, o + 1],
            b_send.at[p, o],
            b_recv.at[p, o],
            2 * behind[o] + h,
        )

    def keep(p):
        return pltpu.make_async_copy(tv.at[p, chip], rc.at[p, 0], local.at[4 + p])

    @pl.loop(0, parents)
    def _(p):
        lt[...] = lv[p].reshape(rank, rank).T

        @pl.loop(0, rows)
        def _(a):
            first = jnp.dot(lt[...], xv[p, a], preferred_element_type=jnp.float32)
            tv[p, :, a] = first.astype(jnp.bfloat16).reshape(CHIPS, per_chip, rank)

        for o in range(CHIPS - 1):
            piece(p, o).start()
        keep(p).start()

    for o in range(CHIPS - 1):
        landed(rv, r_recv, o).wait_recv()
    r_pair = remote(
        rv.at[:, :, h], rv.at[:, :, h], pair_send.at[2], pair_recv.at[2], partner
    )
    r_pair.start()
    own_y.wait()
    y_pair.wait_recv()
    r_pair.wait_recv()

    @pl.loop(0, parents)
    def _(p):
        right = rv[p].reshape(rank, rank)
        for g in range(CHIPS // GROUP):
            if g == 0:
                keep(p).wait()
            slots = range(g * GROUP, (g + 1) * GROUP)
            for s in slots:
                if s:
                    piece(p, s - 1).wait_recv()
            got = rc[p, pl.ds(g * GROUP, GROUP)].reshape(
                GROUP * rows * per_chip, rank
            )
            moved = jnp.dot(got, right, preferred_element_type=jnp.float32)
            sc[0] = moved[:, : rank // 2]
            sc[1] = moved[:, rank // 2 :]
            total = jnp.zeros((GROUP * rows, rank), jnp.float32)
            for k in range(per_chip):
                at = pl.ds(k, GROUP * rows, stride=per_chip)
                second = jnp.concatenate([sc[0, at, :], sc[1, at, :]], axis=1)
                total += jnp.dot(
                    second.astype(jnp.bfloat16),
                    yv[p, k // rows, k % rows],
                    preferred_element_type=jnp.float32,
                )
            part[p, pl.ds(g * GROUP, GROUP)] = total.reshape(GROUP, rows, rank)
            for s in slots:
                if s:
                    give(p, s - 1).start()

    for p in range(parents):
        total = part[p, 0]
        for o in range(CHIPS - 1):
            give(p, o).wait_recv()
            total += ret[p, o + 1]
        o_ref[p] = total

    for copies in (l_copies, r_copies, [y_pair, l_pair, r_pair]):
        for copy in copies:
            copy.wait_send()
    for p in range(parents):
        for o in range(CHIPS - 1):
            piece(p, o).wait_send()
            give(p, o).wait_send()


def shards(core_x, core_y, left, right):
    parents, rows, rank = left.shape
    per_chip = 2 * rows
    bf16, f32 = jnp.bfloat16, jnp.float32
    hops = CHIPS - 1
    dma = pltpu.SemaphoreType.DMA
    return pl.pallas_call(
        kernel,
        out_shape=jax.ShapeDtypeStruct((parents, rows, rank), f32),
        in_specs=[pl.BlockSpec(memory_space=pltpu.HBM)] * 4,
        out_specs=pl.BlockSpec(memory_space=pltpu.VMEM),
        scratch_shapes=[
            pltpu.VMEM((parents, rows, rank, rank), bf16),
            pltpu.VMEM((parents, 2, rows, rank, rank), bf16),
            pltpu.VMEM((parents, CHIPS, 2, rows, rank), bf16),
            pltpu.VMEM((parents, CHIPS, 2, rows, rank), bf16),
            pltpu.VMEM((rank, rank), bf16),
            pltpu.VMEM((parents, CHIPS, rows, per_chip, rank), bf16),
            pltpu.VMEM((parents, CHIPS, rows, per_chip, rank), bf16),
            pltpu.VMEM((2, GROUP * rows * per_chip, rank // 2), f32),
            pltpu.VMEM((parents, CHIPS, rows, rank), f32),
            pltpu.VMEM((parents, CHIPS, rows, rank), f32),
            dma((4 + parents,)),
            dma((3,)),
            dma((3,)),
            dma((hops,)),
            dma((hops,)),
            dma((hops,)),
            dma((hops,)),
            dma((parents, hops)),
            dma((parents, hops)),
            dma((parents, hops)),
            dma((parents, hops)),
        ],
        compiler_params=pltpu.CompilerParams(
            collective_id=0, has_side_effects=True, vmem_limit_bytes=48 << 20
        ),
    )(core_x, core_y, left, right)


def solution(mesh):
    spec4, spec3 = P("node", "cuts", None, None), P("node", "cuts", None)
    return jax.shard_map(
        shards,
        mesh=mesh,
        in_specs=(spec4, spec4, spec3, spec3),
        out_specs=spec3,
        check_vma=False,
    )
```

```python
import jax
import jax.numpy as jnp
from jax import lax
from jax.experimental import pallas as pl
from jax.experimental.pallas import tpu as pltpu
from jax.sharding import PartitionSpec as P

MESH = pl.DeviceIdType.MESH
SIDE = 4
CHIPS = SIDE * SIDE
OFFSETS = (
    (2, 2),
    (2, 1),
    (2, 3),
    (1, 2),
    (3, 2),
    (1, 1),
    (3, 3),
    (1, 3),
    (3, 1),
    (2, 0),
    (0, 2),
    (1, 0),
    (3, 0),
    (0, 1),
    (0, 3),
)
EVERYONE = tuple((dx, dy, dc) for dx, dy in OFFSETS for dc in (0, 1)) + ((0, 0, 1),)
GROUP = 4


def kernel(
    x_hbm,
    y_hbm,
    l_hbm,
    r_hbm,
    o_ref,
    xv,
    yv,
    lr,
    lt,
    tv,
    rc,
    sc,
    own_part,
    part,
    ret,
    local,
    pair_send,
    pair_recv,
    one_send,
    one_recv,
    rest_send,
    rest_recv,
    hand_send,
    hand_recv,
    t_send,
    t_recv,
    b_send,
    b_recv,
):
    parents, rows = x_hbm.shape[0], x_hbm.shape[1]
    rank = x_hbm.shape[2]
    per_chip = 2 * rows
    me = lax.axis_index("cuts")
    h, chip = lax.rem(me, 2), lax.div(me, 2)
    x, y = lax.div(chip, SIDE), lax.rem(chip, SIDE)
    xs = [SIDE * lax.rem(x + d, SIDE) for d in range(SIDE)]
    ys = [lax.rem(y + d, SIDE) for d in range(SIDE)]

    def chip_at(dx, dy):
        return xs[dx % SIDE] + ys[dy % SIDE]

    def remote(src, dst, send, recv, device):
        return pltpu.make_async_remote_copy(
            src_ref=src,
            dst_ref=dst,
            send_sem=send,
            recv_sem=recv,
            device_id={"cuts": device},
            device_id_type=MESH,
        )

    partner = chip * 2 + 1 - h
    ahead = [chip_at(dx, dy) for dx, dy in OFFSETS]
    behind = [chip_at(SIDE - dx, SIDE - dy) for dx, dy in OFFSETS]

    own_l = pltpu.make_async_copy(l_hbm, lr.at[pl.ds(0, parents), chip, h], local.at[0])
    own_r = pltpu.make_async_copy(r_hbm, lr.at[pl.ds(parents, parents), chip, h], local.at[1])
    own_x = pltpu.make_async_copy(x_hbm, xv, local.at[2])
    own_y = pltpu.make_async_copy(y_hbm, yv.at[:, h], local.at[3])
    for copy in (own_l, own_r, own_x, own_y):
        copy.start()

    first_plane = lax.axis_index("node") == 0
    absent = jnp.where(first_plane, 0, -1)
    late = jnp.logical_and(first_plane, me == 0)
    helper = jnp.logical_and(first_plane, me == 1)
    others = [
        (2 * chip_at(dx, dy) + (1 - h if dc else h), dc) for dx, dy, dc in EVERYONE
    ]
    barrier = pltpu.get_barrier_semaphore()

    @pl.when(jnp.logical_not(late))
    def _():
        for to, _ in others:
            pl.semaphore_signal(
                barrier, inc=1, device_id={"cuts": to}, device_id_type=MESH
            )

    met = jnp.logical_or(late, jnp.logical_not(first_plane))
    pl.semaphore_wait(barrier, jnp.where(met, len(others), len(others) - 1))

    later = pl.ds(1, 2 * parents - 1)

    def one(o):
        to, dc = others[o]
        mine = lr.at[0, chip, h]
        return remote(mine, mine, one_send.at[dc], one_recv.at[dc], to)

    def ones(count, dc):
        blocks = lr.at[0, pl.ds(CHIPS - count, count), 0]
        return remote(blocks, blocks, one_send.at[dc], one_recv.at[dc], partner)

    def rest(o):
        mine = lr.at[later, chip, h]
        return remote(
            mine, mine, rest_send.at[0], rest_recv.at[0], 2 * ahead[o] + h
        )

    def rests():
        blocks = lr.at[later, pl.ds(1, CHIPS - 1), 0]
        return remote(blocks, blocks, rest_send.at[0], rest_recv.at[0], partner)

    def rest_pair():
        rows_of = lr.at[later, :, h]
        return remote(rows_of, rows_of, pair_send.at[0], pair_recv.at[0], partner)

    def hand():
        own, most = lr.at[0, 0, 1], lr.at[0, pl.ds(1, CHIPS - 1)]
        return (
            remote(own, own, hand_send.at[0], hand_recv.at[0], 0),
            remote(most, most, hand_send.at[1], hand_recv.at[1], 0),
        )

    y_pair = [
        remote(
            y_hbm.at[p],
            yv.at[p, h],
            pair_send.at[1 + p],
            pair_recv.at[1 + p],
            partner,
        )
        for p in range(parents)
    ]

    own_l.wait()
    for o in range(len(others)):

        @pl.when(others[o][0] != absent)
        def _():
            one(o).start()

    own_r.wait()
    for o in range(CHIPS - 1):

        @pl.when(2 * ahead[o] + h != absent)
        def _():
            rest(o).start()

    @pl.when(partner != absent)
    def _():
        for copy in y_pair:
            copy.start()

    @pl.when(jnp.logical_not(late))
    def _():
        ones(CHIPS - 1, 0).wait_recv()
        ones(CHIPS, 1).wait_recv()

    @pl.when(helper)
    def _():
        for copy in hand() + tuple(y_pair):
            copy.start()

    @pl.when(late)
    def _():
        for copy in hand():
            copy.wait_recv()

    for o in range(CHIPS - 1):

        @pl.when(2 * ahead[o] + h == absent)
        def _():
            rest(o).start()

    def piece(p, o):
        return remote(
            tv.at[p, ahead[o]],
            rc.at[p, o + 1],
            t_send.at[p],
            t_recv.at[p, (o + 1) // GROUP],
            2 * ahead[o] + h,
        )

    def pieces(p, g):
        slots = pl.ds(max(g * GROUP, 1), GROUP - (g == 0))
        return remote(
            rc.at[p, slots], rc.at[p, slots], t_send.at[p], t_recv.at[p, g], partner
        )

    def give(p, o):
        return remote(
            part.at[p, o + 1],
            ret.at[p, o + 1],
            b_send.at[p],
            b_recv.at[p],
            2 * behind[o] + h,
        )

    def all_of(ref, send, recv, p):
        blocks = ref.at[p, pl.ds(1, CHIPS - 1)]
        return remote(blocks, blocks, send.at[p], recv.at[p], partner)

    def keep(p):
        return pltpu.make_async_copy(tv.at[p, chip], rc.at[p, 0], local.at[4 + p])

    own_x.wait()
    for p in range(parents):
        lt[...] = lr[p].reshape(rank, rank).T

        @pl.loop(0, rows)
        def _(a):
            first = jnp.dot(lt[...], xv[p, a], preferred_element_type=jnp.float32)
            tv[p, :, a] = first.astype(jnp.bfloat16).reshape(CHIPS, per_chip, rank)

        for o in range(CHIPS - 1):
            piece(p, o).start()
        keep(p).start()
        if p == 0:
            rests().wait_recv()
            rest_pair().start()
            rest_pair().wait_recv()

    own_y.wait()
    for copy in y_pair:
        copy.wait_recv()

    skips = [jnp.logical_and(first_plane, jnp.logical_and(h == dc, me != 0)) for dc in (0, 1)]
    for dc in (0, 1):

        @pl.when(skips[dc])
        def _():
            ones(CHIPS - 2 + dc, dc).wait_send()

        @pl.when(jnp.logical_not(skips[dc]))
        def _():
            ones(CHIPS - 1 + dc, dc).wait_send()

    rests().wait_send()
    rest_pair().wait_send()
    for copy in y_pair:
        copy.wait_send()

    @pl.when(helper)
    def _():
        for copy in hand():
            copy.wait_send()

    @pl.loop(0, parents)
    def _(p):
        weights = lr[parents + p].reshape(rank, rank)
        for g in range(CHIPS // GROUP):
            if g == 0:
                keep(p).wait()
            slots = range(g * GROUP, (g + 1) * GROUP)
            pieces(p, g).wait_recv()
            got = rc[p, pl.ds(g * GROUP, GROUP)].reshape(
                GROUP * rows * per_chip, rank
            )
            moved = jnp.dot(got, weights, preferred_element_type=jnp.float32)
            sc[0] = moved[:, : rank // 2]
            sc[1] = moved[:, rank // 2 :]
            total = jnp.zeros((GROUP * rows, rank), jnp.float32)
            for k in range(per_chip):
                at = pl.ds(k, GROUP * rows, stride=per_chip)
                second = jnp.concatenate([sc[0, at, :], sc[1, at, :]], axis=1)
                total += jnp.dot(
                    second.astype(jnp.bfloat16),
                    yv[p, k // rows, k % rows],
                    preferred_element_type=jnp.float32,
                )
            whole = total.reshape(GROUP, rows, rank)
            if g == 0:
                own_part[p] = whole[0]
            part[p, pl.ds(g * GROUP, GROUP)] = whole.astype(jnp.bfloat16)
            for s in slots:
                if s:
                    give(p, s - 1).start()

    for p in range(parents):
        all_of(ret, b_send, b_recv, p).wait_recv()
        returned = ret[p, pl.ds(1, CHIPS - 1)].astype(jnp.float32)
        o_ref[p] = own_part[p] + jnp.sum(returned, axis=0)

    for p in range(parents):
        all_of(tv, t_send, b_recv, p).wait_send()
        all_of(part, b_send, b_recv, p).wait_send()


def shards(*arrays):
    parents, rows, rank = arrays[2].shape
    per_chip = 2 * rows
    bf16, f32 = jnp.bfloat16, jnp.float32
    dma = pltpu.SemaphoreType.DMA
    return pl.pallas_call(
        kernel,
        out_shape=jax.ShapeDtypeStruct((parents, rows, rank), f32),
        in_specs=[pl.BlockSpec(memory_space=pltpu.HBM)] * 4,
        out_specs=pl.BlockSpec(memory_space=pltpu.VMEM),
        scratch_shapes=[
            pltpu.VMEM((parents, rows, rank, rank), bf16),
            pltpu.VMEM((parents, 2, rows, rank, rank), bf16),
            pltpu.VMEM((2 * parents, CHIPS, 2, rows, rank), bf16),
            pltpu.VMEM((rank, rank), bf16),
            pltpu.VMEM((parents, CHIPS, rows, per_chip, rank), bf16),
            pltpu.VMEM((parents, CHIPS, rows, per_chip, rank), bf16),
            pltpu.VMEM((2, GROUP * rows * per_chip, rank // 2), f32),
            pltpu.VMEM((parents, rows, rank), f32),
            pltpu.VMEM((parents, CHIPS, rows, rank), bf16),
            pltpu.VMEM((parents, CHIPS, rows, rank), bf16),
            dma((4 + parents,)),
            dma((1 + parents,)),
            dma((1 + parents,)),
            dma((2,)),
            dma((2,)),
            dma((1,)),
            dma((1,)),
            dma((2,)),
            dma((2,)),
            dma((parents,)),
            dma((parents, CHIPS // GROUP)),
            dma((parents,)),
            dma((parents,)),
        ],
        compiler_params=pltpu.CompilerParams(
            collective_id=0, has_side_effects=True, vmem_limit_bytes=48 << 20
        ),
    )(*(pltpu.with_memory_space_constraint(v, pltpu.HBM) for v in arrays))


def solution(mesh):
    spec4, spec3 = P("node", "cuts", None, None), P("node", "cuts", None)
    return jax.shard_map(
        shards,
        mesh=mesh,
        in_specs=(spec4, spec4, spec3, spec3),
        out_specs=spec3,
        check_vma=False,
    )
```

```python
import jax
import jax.numpy as jnp
from jax import lax
from jax.experimental import pallas as pl
from jax.experimental.pallas import tpu as pltpu
from jax.sharding import PartitionSpec as P

MESH = pl.DeviceIdType.MESH
SIDE = 4
CHIPS = SIDE * SIDE
OFFSETS = (
    (2, 2),
    (2, 1),
    (2, 3),
    (1, 2),
    (3, 2),
    (1, 1),
    (3, 3),
    (1, 3),
    (3, 1),
    (2, 0),
    (0, 2),
    (1, 0),
    (3, 0),
    (0, 1),
    (0, 3),
)
EVERYONE = tuple((dx, dy, dc) for dx, dy in OFFSETS for dc in (0, 1)) + ((0, 0, 1),)
GROUP = 4


def kernel(
    x_hbm,
    y_hbm,
    l_hbm,
    r_hbm,
    o_ref,
    xv,
    yv,
    lr,
    lt,
    tv,
    rc,
    sc,
    own_part,
    part,
    ret,
    local,
    pair_send,
    pair_recv,
    one_send,
    one_recv,
    rest_send,
    rest_recv,
    hand_send,
    hand_recv,
    t_send,
    t_recv,
    b_send,
    b_recv,
):
    parents, rows = x_hbm.shape[0], x_hbm.shape[1]
    rank = x_hbm.shape[2]
    per_chip = 2 * rows
    me = lax.axis_index("cuts")
    h, chip = lax.rem(me, 2), lax.div(me, 2)
    x, y = lax.div(chip, SIDE), lax.rem(chip, SIDE)
    xs = [SIDE * lax.rem(x + d, SIDE) for d in range(SIDE)]
    ys = [lax.rem(y + d, SIDE) for d in range(SIDE)]

    def chip_at(dx, dy):
        return xs[dx % SIDE] + ys[dy % SIDE]

    def remote(src, dst, send, recv, device):
        return pltpu.make_async_remote_copy(
            src_ref=src,
            dst_ref=dst,
            send_sem=send,
            recv_sem=recv,
            device_id={"cuts": device},
            device_id_type=MESH,
        )

    partner = chip * 2 + 1 - h
    ahead = [chip_at(dx, dy) for dx, dy in OFFSETS]
    behind = [chip_at(SIDE - dx, SIDE - dy) for dx, dy in OFFSETS]

    own_l = pltpu.make_async_copy(l_hbm, lr.at[pl.ds(0, parents), chip, h], local.at[0])
    own_r = pltpu.make_async_copy(r_hbm, lr.at[pl.ds(parents, parents), chip, h], local.at[1])
    own_x = pltpu.make_async_copy(x_hbm, xv, local.at[2])
    own_y = pltpu.make_async_copy(y_hbm, yv.at[:, h], local.at[3])
    for copy in (own_l, own_r, own_x, own_y):
        copy.start()

    first_plane = lax.axis_index("node") == 0
    absent = jnp.where(first_plane, 0, -1)
    late = jnp.logical_and(first_plane, me == 0)
    helper = jnp.logical_and(first_plane, me == 1)
    others = [
        (2 * chip_at(dx, dy) + (1 - h if dc else h), dc) for dx, dy, dc in EVERYONE
    ]
    barrier = pltpu.get_barrier_semaphore()

    @pl.when(jnp.logical_not(late))
    def _():
        for to, _ in others:
            pl.semaphore_signal(
                barrier, inc=1, device_id={"cuts": to}, device_id_type=MESH
            )

    met = jnp.logical_or(late, jnp.logical_not(first_plane))
    pl.semaphore_wait(barrier, jnp.where(met, len(others), len(others) - 1))

    later = pl.ds(1, 2 * parents - 1)

    def one(o):
        to, dc = others[o]
        mine = lr.at[0, chip, h]
        return remote(mine, mine, one_send.at[dc], one_recv.at[dc], to)

    def ones(count, dc):
        blocks = lr.at[0, pl.ds(CHIPS - count, count), 0]
        return remote(blocks, blocks, one_send.at[dc], one_recv.at[dc], partner)

    def rest(o):
        mine = lr.at[later, chip, h]
        return remote(
            mine, mine, rest_send.at[0], rest_recv.at[0], 2 * ahead[o] + h
        )

    def rests():
        blocks = lr.at[later, pl.ds(1, CHIPS - 1), 0]
        return remote(blocks, blocks, rest_send.at[0], rest_recv.at[0], partner)

    def rest_pair():
        rows_of = lr.at[later, :, h]
        return remote(rows_of, rows_of, pair_send.at[0], pair_recv.at[0], partner)

    def hand():
        own, most = lr.at[0, 0, 1], lr.at[0, pl.ds(1, CHIPS - 1)]
        return (
            remote(own, own, hand_send.at[0], hand_recv.at[0], 0),
            remote(most, most, hand_send.at[1], hand_recv.at[1], 0),
        )

    y_pair = [
        remote(
            y_hbm.at[p],
            yv.at[p, h],
            pair_send.at[1 + p],
            pair_recv.at[1 + p],
            partner,
        )
        for p in range(parents)
    ]

    own_l.wait()
    for o in range(len(others)):

        @pl.when(others[o][0] != absent)
        def _():
            one(o).start()

    own_r.wait()
    for o in range(CHIPS - 1):

        @pl.when(2 * ahead[o] + h != absent)
        def _():
            rest(o).start()

    @pl.when(partner != absent)
    def _():
        for copy in y_pair:
            copy.start()

    @pl.when(jnp.logical_not(late))
    def _():
        ones(CHIPS - 1, 0).wait_recv()
        ones(CHIPS, 1).wait_recv()

    @pl.when(helper)
    def _():
        for copy in hand() + tuple(y_pair):
            copy.start()

    @pl.when(late)
    def _():
        for copy in hand():
            copy.wait_recv()

    for o in range(CHIPS - 1):

        @pl.when(2 * ahead[o] + h == absent)
        def _():
            rest(o).start()

    half = rows // 2

    def piece(p, o, part_of):
        some = pl.ds(part_of * half, half)
        return remote(
            tv.at[p, ahead[o], some],
            rc.at[p, o + 1, some],
            t_send.at[p],
            t_recv.at[p, (o + 1) // GROUP],
            2 * ahead[o] + h,
        )

    def pieces(p, g):
        slots = pl.ds(max(g * GROUP, 1), GROUP - (g == 0))
        return remote(
            rc.at[p, slots], rc.at[p, slots], t_send.at[p], t_recv.at[p, g], partner
        )

    def give(p, o):
        return remote(
            part.at[p, o + 1],
            ret.at[p, o + 1],
            b_send.at[p],
            b_recv.at[p],
            2 * behind[o] + h,
        )

    def all_of(ref, send, recv, p):
        blocks = ref.at[p, pl.ds(1, CHIPS - 1)]
        return remote(blocks, blocks, send.at[p], recv.at[p], partner)

    def keep(p):
        return pltpu.make_async_copy(tv.at[p, chip], rc.at[p, 0], local.at[4 + p])

    own_x.wait()
    for p in range(parents):
        lt[...] = lr[p].reshape(rank, rank).T

        for part_of in range(2):
            for a in range(part_of * half, (part_of + 1) * half):
                first = jnp.dot(lt[...], xv[p, a], preferred_element_type=jnp.float32)
                tv[p, :, a] = first.astype(jnp.bfloat16).reshape(CHIPS, per_chip, rank)
            for o in range(CHIPS - 1):
                piece(p, o, part_of).start()

        keep(p).start()
        if p == 0:
            rests().wait_recv()
            rest_pair().start()
            rest_pair().wait_recv()

    own_y.wait()
    for copy in y_pair:
        copy.wait_recv()

    skips = [jnp.logical_and(first_plane, jnp.logical_and(h == dc, me != 0)) for dc in (0, 1)]
    for dc in (0, 1):

        @pl.when(skips[dc])
        def _():
            ones(CHIPS - 2 + dc, dc).wait_send()

        @pl.when(jnp.logical_not(skips[dc]))
        def _():
            ones(CHIPS - 1 + dc, dc).wait_send()

    rests().wait_send()
    rest_pair().wait_send()
    for copy in y_pair:
        copy.wait_send()

    @pl.when(helper)
    def _():
        for copy in hand():
            copy.wait_send()

    @pl.loop(0, parents)
    def _(p):
        weights = lr[parents + p].reshape(rank, rank)
        for g in range(CHIPS // GROUP):
            if g == 0:
                keep(p).wait()
            slots = range(g * GROUP, (g + 1) * GROUP)
            pieces(p, g).wait_recv()
            got = rc[p, pl.ds(g * GROUP, GROUP)].reshape(
                GROUP * rows * per_chip, rank
            )
            moved = jnp.dot(got, weights, preferred_element_type=jnp.float32)
            sc[0] = moved[:, : rank // 2]
            sc[1] = moved[:, rank // 2 :]
            total = jnp.zeros((GROUP * rows, rank), jnp.float32)
            for k in range(per_chip):
                at = pl.ds(k, GROUP * rows, stride=per_chip)
                second = jnp.concatenate([sc[0, at, :], sc[1, at, :]], axis=1)
                total += jnp.dot(
                    second.astype(jnp.bfloat16),
                    yv[p, k // rows, k % rows],
                    preferred_element_type=jnp.float32,
                )
            whole = total.reshape(GROUP, rows, rank)
            if g == 0:
                own_part[p] = whole[0]
            part[p, pl.ds(g * GROUP, GROUP)] = whole.astype(jnp.bfloat16)
            for s in slots:
                if s:
                    give(p, s - 1).start()

    for p in range(parents):
        all_of(ret, b_send, b_recv, p).wait_recv()
        returned = ret[p, pl.ds(1, CHIPS - 1)].astype(jnp.float32)
        o_ref[p] = own_part[p] + jnp.sum(returned, axis=0)

    for p in range(parents):
        all_of(tv, t_send, b_recv, p).wait_send()
        all_of(part, b_send, b_recv, p).wait_send()


def shards(*arrays):
    parents, rows, rank = arrays[2].shape
    per_chip = 2 * rows
    bf16, f32 = jnp.bfloat16, jnp.float32
    dma = pltpu.SemaphoreType.DMA
    return pl.pallas_call(
        kernel,
        out_shape=jax.ShapeDtypeStruct((parents, rows, rank), f32),
        in_specs=[pl.BlockSpec(memory_space=pltpu.HBM)] * 4,
        out_specs=pl.BlockSpec(memory_space=pltpu.VMEM),
        scratch_shapes=[
            pltpu.VMEM((parents, rows, rank, rank), bf16),
            pltpu.VMEM((parents, 2, rows, rank, rank), bf16),
            pltpu.VMEM((2 * parents, CHIPS, 2, rows, rank), bf16),
            pltpu.VMEM((rank, rank), bf16),
            pltpu.VMEM((parents, CHIPS, rows, per_chip, rank), bf16),
            pltpu.VMEM((parents, CHIPS, rows, per_chip, rank), bf16),
            pltpu.VMEM((2, GROUP * rows * per_chip, rank // 2), f32),
            pltpu.VMEM((parents, rows, rank), f32),
            pltpu.VMEM((parents, CHIPS, rows, rank), bf16),
            pltpu.VMEM((parents, CHIPS, rows, rank), bf16),
            dma((4 + parents,)),
            dma((1 + parents,)),
            dma((1 + parents,)),
            dma((2,)),
            dma((2,)),
            dma((1,)),
            dma((1,)),
            dma((2,)),
            dma((2,)),
            dma((parents,)),
            dma((parents, CHIPS // GROUP)),
            dma((parents,)),
            dma((parents,)),
        ],
        compiler_params=pltpu.CompilerParams(
            collective_id=0, has_side_effects=True, vmem_limit_bytes=48 << 20
        ),
    )(*(pltpu.with_memory_space_constraint(v, pltpu.HBM) for v in arrays))


def solution(mesh):
    spec4, spec3 = P("node", "cuts", None, None), P("node", "cuts", None)
    return jax.shard_map(
        shards,
        mesh=mesh,
        in_specs=(spec4, spec4, spec3, spec3),
        out_specs=spec3,
        check_vma=False,
    )
```

```python
import jax
import jax.numpy as jnp
from jax import lax
from jax.experimental import pallas as pl
from jax.experimental.pallas import tpu as pltpu
from jax.sharding import PartitionSpec as P

MESH = pl.DeviceIdType.MESH
SIDE = 4
CHIPS = SIDE * SIDE
OFFSETS = (
    (2, 2),
    (2, 1),
    (2, 3),
    (1, 2),
    (3, 2),
    (1, 1),
    (3, 3),
    (1, 3),
    (3, 1),
    (2, 0),
    (0, 2),
    (1, 0),
    (3, 0),
    (0, 1),
    (0, 3),
)
EVERYONE = ((0, 0, 1),) + tuple((dx, dy, dc) for dx, dy in OFFSETS for dc in (0, 1))
GROUP = 4
HELD = 4
HOLD_AFTER = 3


def kernel(
    x_hbm,
    y_hbm,
    l_hbm,
    r_hbm,
    o_ref,
    xv,
    yv,
    lr,
    lt,
    tv,
    rc,
    sc,
    own_part,
    part,
    ret,
    local,
    pair_send,
    pair_recv,
    one_send,
    one_recv,
    rest_send,
    rest_recv,
    hand_send,
    hand_recv,
    t_send,
    t_recv,
    b_send,
    b_recv,
):
    parents, rows = x_hbm.shape[0], x_hbm.shape[1]
    rank = x_hbm.shape[2]
    per_chip = 2 * rows
    me = lax.axis_index("cuts")
    h, chip = lax.rem(me, 2), lax.div(me, 2)
    x, y = lax.div(chip, SIDE), lax.rem(chip, SIDE)
    xs = [SIDE * lax.rem(x + d, SIDE) for d in range(SIDE)]
    ys = [lax.rem(y + d, SIDE) for d in range(SIDE)]

    def chip_at(dx, dy):
        return xs[dx % SIDE] + ys[dy % SIDE]

    def remote(src, dst, send, recv, device):
        return pltpu.make_async_remote_copy(
            src_ref=src,
            dst_ref=dst,
            send_sem=send,
            recv_sem=recv,
            device_id={"cuts": device},
            device_id_type=MESH,
        )

    partner = chip * 2 + 1 - h
    ahead = [chip_at(dx, dy) for dx, dy in OFFSETS]
    behind = [chip_at(SIDE - dx, SIDE - dy) for dx, dy in OFFSETS]

    first_plane = lax.axis_index("node") == 0
    absent = jnp.where(first_plane, 0, -1)
    late = jnp.logical_and(first_plane, me == 0)
    helper = jnp.logical_and(first_plane, me == 1)
    hold = jnp.logical_not(first_plane)
    others = [
        (2 * chip_at(dx, dy) + (1 - h if dc else h), dc) for dx, dy, dc in EVERYONE
    ]
    barrier = pltpu.get_barrier_semaphore()

    @pl.when(jnp.logical_not(late))
    def _():
        for to, _ in others:
            pl.semaphore_signal(
                barrier, inc=1, device_id={"cuts": to}, device_id_type=MESH
            )

    own_l = pltpu.make_async_copy(l_hbm, lr.at[pl.ds(0, parents), h, chip], local.at[0])
    own_r = pltpu.make_async_copy(r_hbm, lr.at[pl.ds(parents, parents), h, chip], local.at[1])
    own_x = pltpu.make_async_copy(x_hbm, xv, local.at[2])
    own_y = pltpu.make_async_copy(y_hbm, yv.at[:, h], local.at[3])
    for copy in (own_l, own_r, own_x, own_y):
        copy.start()

    met = jnp.logical_or(late, jnp.logical_not(first_plane))
    pl.semaphore_wait(barrier, jnp.where(met, len(others), len(others) - 1))

    later = pl.ds(1, 2 * parents - 1)

    def one(o):
        to, dc = others[o]
        mine = lr.at[0, h, chip]
        return remote(mine, mine, one_send.at[dc], one_recv.at[dc], to)

    def matrix(i):
        return jnp.swapaxes(lr[i], 0, 1).reshape(rank, rank)

    def ones(count, dc):
        blocks = lr.at[0, 0, pl.ds(CHIPS - count, count)]
        return remote(blocks, blocks, one_send.at[dc], one_recv.at[dc], partner)

    def rest(o):
        mine = lr.at[later, h, chip]
        return remote(
            mine, mine, rest_send.at[0], rest_recv.at[0], 2 * ahead[o] + h
        )

    def rests():
        blocks = lr.at[later, 0, pl.ds(1, CHIPS - 1)]
        return remote(blocks, blocks, rest_send.at[0], rest_recv.at[0], partner)

    def rest_pair():
        rows_of = lr.at[later, h]
        return remote(rows_of, rows_of, pair_send.at[0], pair_recv.at[0], partner)

    def hand():
        own, most = lr.at[0, 1, 0], lr.at[0, :, pl.ds(1, CHIPS - 1)]
        return (
            remote(own, own, hand_send.at[0], hand_recv.at[0], 0),
            remote(most, most, hand_send.at[1], hand_recv.at[1], 0),
        )

    y_pair = [
        remote(
            y_hbm.at[p],
            yv.at[p, h],
            pair_send.at[1 + p],
            pair_recv.at[1 + p],
            partner,
        )
        for p in range(parents)
    ]

    own_l.wait()
    for o in range(len(others)):

        @pl.when(others[o][0] != absent)
        def _():
            one(o).start()

    own_r.wait()
    for o in range(CHIPS - 1):

        @pl.when(2 * ahead[o] + h != absent)
        def _():
            rest(o).start()

    @pl.when(partner != absent)
    def _():
        for copy in y_pair:
            copy.start()

    @pl.when(jnp.logical_not(late))
    def _():
        ones(CHIPS - 1, 0).wait_recv()
        ones(CHIPS, 1).wait_recv()

    @pl.when(helper)
    def _():
        for copy in hand() + tuple(y_pair):
            copy.start()

    @pl.when(late)
    def _():
        for copy in hand():
            copy.wait_recv()

    for o in range(CHIPS - 1):

        @pl.when(2 * ahead[o] + h == absent)
        def _():
            rest(o).start()

    half = rows // 2

    def piece(p, o, part_of):
        some = pl.ds(part_of * half, half)
        return remote(
            tv.at[p, ahead[o], some],
            rc.at[p, o + 1, some],
            t_send.at[p],
            t_recv.at[p, (o + 1) // GROUP],
            2 * ahead[o] + h,
        )

    def pieces(p, g):
        slots = pl.ds(max(g * GROUP, 1), GROUP - (g == 0))
        return remote(
            rc.at[p, slots], rc.at[p, slots], t_send.at[p], t_recv.at[p, g], partner
        )

    def give(p, o):
        return remote(
            part.at[p, o + 1],
            ret.at[p, o + 1],
            b_send.at[p],
            b_recv.at[p],
            2 * behind[o] + h,
        )

    def all_of(ref, send, recv, p):
        blocks = ref.at[p, pl.ds(1, CHIPS - 1)]
        return remote(blocks, blocks, send.at[p], recv.at[p], partner)

    def keep(p):
        return pltpu.make_async_copy(tv.at[p, chip], rc.at[p, 0], local.at[4 + p])

    own_x.wait()
    for p in range(parents):
        lt[...] = matrix(p).T

        for part_of in range(2):
            for a in range(part_of * half, (part_of + 1) * half):
                first = jnp.dot(lt[...], xv[p, a], preferred_element_type=jnp.float32)
                tv[p, :, a] = first.astype(jnp.bfloat16).reshape(CHIPS, per_chip, rank)
            if p == 0 and part_of == 1:
                rests().wait_recv()
                rest_pair().start()
            for o in range(CHIPS - 1 if p == 0 else CHIPS - 1 - HELD):
                piece(p, o, part_of).start()
            if p == parents - 1:

                @pl.when(jnp.logical_not(hold))
                def _():
                    for o in range(CHIPS - 1 - HELD, CHIPS - 1):
                        piece(p, o, part_of).start()

        keep(p).start()
        if p == 0:
            rest_pair().wait_recv()

    own_y.wait()
    for copy in y_pair:
        copy.wait_recv()

    skips = [jnp.logical_and(first_plane, jnp.logical_and(h == dc, me != 0)) for dc in (0, 1)]
    for dc in (0, 1):

        @pl.when(skips[dc])
        def _():
            ones(CHIPS - 2 + dc, dc).wait_send()

        @pl.when(jnp.logical_not(skips[dc]))
        def _():
            ones(CHIPS - 1 + dc, dc).wait_send()

    rests().wait_send()
    rest_pair().wait_send()
    for copy in y_pair:
        copy.wait_send()

    @pl.when(helper)
    def _():
        for copy in hand():
            copy.wait_send()

    @pl.loop(0, parents)
    def _(p):
        weights = matrix(parents + p)
        for g in range(CHIPS // GROUP):
            if g == 0:
                keep(p).wait()
            slots = range(g * GROUP, (g + 1) * GROUP)
            pieces(p, g).wait_recv()
            got = rc[p, pl.ds(g * GROUP, GROUP)].reshape(
                GROUP * rows * per_chip, rank
            )
            moved = jnp.dot(got, weights, preferred_element_type=jnp.float32)
            sc[0] = moved[:, : rank // 2]
            sc[1] = moved[:, rank // 2 :]
            total = jnp.zeros((GROUP * rows, rank), jnp.float32)
            for k in range(per_chip):
                at = pl.ds(k, GROUP * rows, stride=per_chip)
                second = jnp.concatenate([sc[0, at, :], sc[1, at, :]], axis=1)
                total += jnp.dot(
                    second.astype(jnp.bfloat16),
                    yv[p, k // rows, k % rows],
                    preferred_element_type=jnp.float32,
                )
            whole = total.reshape(GROUP, rows, rank)
            if g == 0:
                own_part[p] = whole[0]
            part[p, pl.ds(g * GROUP, GROUP)] = whole.astype(jnp.bfloat16)
            for s in slots:
                if s:
                    give(p, s - 1).start()
            if g == HOLD_AFTER:

                @pl.when(jnp.logical_and(p == 0, hold))
                def _():
                    for o in range(CHIPS - 1 - HELD, CHIPS - 1):
                        for part_of in range(2):
                            piece(parents - 1, o, part_of).start()


    for p in range(parents):
        all_of(ret, b_send, b_recv, p).wait_recv()
        returned = ret[p, pl.ds(1, CHIPS - 1)].astype(jnp.float32)
        o_ref[p] = own_part[p] + jnp.sum(returned, axis=0)

    for p in range(parents):
        all_of(tv, t_send, b_recv, p).wait_send()
        all_of(part, b_send, b_recv, p).wait_send()


def shards(*arrays):
    parents, rows, rank = arrays[2].shape
    per_chip = 2 * rows
    bf16, f32 = jnp.bfloat16, jnp.float32
    dma = pltpu.SemaphoreType.DMA
    return pl.pallas_call(
        kernel,
        out_shape=jax.ShapeDtypeStruct((parents, rows, rank), f32),
        in_specs=[pl.BlockSpec(memory_space=pltpu.HBM)] * 4,
        out_specs=pl.BlockSpec(memory_space=pltpu.VMEM),
        scratch_shapes=[
            pltpu.VMEM((parents, rows, rank, rank), bf16),
            pltpu.VMEM((parents, 2, rows, rank, rank), bf16),
            pltpu.VMEM((2 * parents, 2, CHIPS, rows, rank), bf16),
            pltpu.VMEM((rank, rank), bf16),
            pltpu.VMEM((parents, CHIPS, rows, per_chip, rank), bf16),
            pltpu.VMEM((parents, CHIPS, rows, per_chip, rank), bf16),
            pltpu.VMEM((2, GROUP * rows * per_chip, rank // 2), f32),
            pltpu.VMEM((parents, rows, rank), f32),
            pltpu.VMEM((parents, CHIPS, rows, rank), bf16),
            pltpu.VMEM((parents, CHIPS, rows, rank), bf16),
            dma((4 + parents,)),
            dma((1 + parents,)),
            dma((1 + parents,)),
            dma((2,)),
            dma((2,)),
            dma((1,)),
            dma((1,)),
            dma((2,)),
            dma((2,)),
            dma((parents,)),
            dma((parents, CHIPS // GROUP)),
            dma((parents,)),
            dma((parents,)),
        ],
        compiler_params=pltpu.CompilerParams(
            collective_id=0, has_side_effects=True, vmem_limit_bytes=48 << 20
        ),
    )(*(pltpu.with_memory_space_constraint(v, pltpu.HBM) for v in arrays))


def solution(mesh):
    spec4, spec3 = P("node", "cuts", None, None), P("node", "cuts", None)
    return jax.shard_map(
        shards,
        mesh=mesh,
        in_specs=(spec4, spec4, spec3, spec3),
        out_specs=spec3,
        check_vma=False,
    )
```
